128 devices in a mesh: group: 4 (over x_hi, core), site: 32 (over x_lo, z, y).
Axes of the slice: x: 4 (x_hi: 2, x_lo: 2; x = x_hi * 2 + x_lo), y: 4, z: 4, core: 2. Of those that a mesh axis runs over, the one named last changes fastest.
Arguments:
- residual_in: bfloat16 [32, 64, 128, 128], P('site', 'group'), may hold values from -6 to 6
- self_block: bfloat16 [32, 64, 64, 128], P('site'), may hold values from -0.25 to 0.25
- hop_blocks: bfloat16 [32, 64, 8, 64, 128], P('site'), may hold values from -0.1875 to 0.1875
Outputs:
- correction: float32 [32, 64, 128, 128], P('site', 'group')
- residual_out: float32 [32, 64, 128, 128], P('site', 'group')
The draws below stay inside these ranges and needn't reach their ends.
All inputs are finite; a program needn't handle non-finite values.
Results may differ from the reference program's by a relative error of at most 0.017.
Values may be sent and summed in bfloat16 or wider, within the bound.
A program may use at most 64 MiB of HBM per device.

```python
import jax
import jax.numpy as jnp
from jax import lax

C = 64
RHS = 128
LY = 4
LZ = 2
STEPS = 4
X = 8
SPATIAL = 64
NT = 32


def levels(own_key, shape, split, low, high):
    def one(axis_at, blocks):
        steps = jax.random.uniform(jax.random.fold_in(jax.random.fold_in(own_key, 6), axis_at), (blocks,), jnp.float32, low / len(split), high / len(split))
        return jnp.repeat(jnp.exp(steps), shape[axis_at] // blocks).reshape((-1,) + (1,) * (len(shape) - axis_at - 1))

    level = one(*split[0])
    for cut in split[1:]:
        level = level * one(*cut)
    return level


def gaussian(rng, extent, scale, bound, shards=(), kind=jnp.bfloat16):
    gain = levels(rng, extent, shards, -0.22, 0.18) if shards else 1.0
    values = jax.random.normal(rng, extent, jnp.float32) * scale * gain
    return jnp.minimum(jnp.maximum(values, -bound), bound).astype(kind)


def setup_inputs(seed: int = 0) -> dict:
    arg_keys = jax.random.split(jax.random.key(seed), 4)
    return {
        "residual_in": gaussian(arg_keys[0], (NT, SPATIAL, RHS, 2 * C), 1.0, 6.0, ((0, 32), (1, 4))),
        "self_block": gaussian(arg_keys[1], (NT, SPATIAL, C, 2 * C), (8 * C) ** -0.5, 0.25, ((0, 32),)),
        "hop_blocks": gaussian(arg_keys[2], (NT, SPATIAL, 8, C, 2 * C), (14 * C) ** -0.5, 0.1875, ((0, 32),)),
    }


diagonal_shift = 1.5
center_value = 1.5
half_width = 1.0


def paired(vector):
    half = vector.shape[-1] // 2
    real_part = vector[..., :half]
    imag_part = vector[..., half:]
    conjugate = jnp.concatenate([real_part, -imag_part], axis=-1)
    swapped = jnp.concatenate([imag_part, real_part], axis=-1)
    return jnp.concatenate([conjugate, swapped], axis=-2)


def operate(vector, self_block, hop_blocks):
    grid = vector.reshape(NT, X, LY, LZ, RHS, 2 * C)
    moved = []
    for axis_number in (1, 2, 3, 0):
        moved.append(jnp.roll(grid, -1, axis_number).reshape(NT, SPATIAL, RHS, 2 * C))
        moved.append(jnp.roll(grid, 1, axis_number).reshape(NT, SPATIAL, RHS, 2 * C))
    stacked = jnp.stack(moved, axis=2)

    def one_slice(items):
        own, around, self_part, hop_part = items
        own_out = jnp.einsum('sab,skb->ska', self_part.astype(jnp.float32), paired(own).astype(jnp.float32))
        hop_out = jnp.einsum('smab,smkb->ska', hop_part.astype(jnp.float32), paired(around).astype(jnp.float32))
        total = own_out + hop_out
        return jnp.concatenate([total[:, :RHS], total[:, RHS:]], axis=-1)

    applied = lax.map(one_slice, (vector, stacked, self_block, hop_blocks))
    return diagonal_shift * vector.astype(jnp.float32) + applied


def reference(residual_in, self_block, hop_blocks):
    residual = residual_in.astype(jnp.float32)
    correction = jnp.zeros(residual.shape, jnp.float32)
    ratio = half_width / center_value
    direction = residual / center_value
    for number in range(STEPS):
        if number > 0:
            ratio_next = 1.0 / (2.0 * center_value / half_width - ratio)
            direction = ratio_next * ratio * direction + (2.0 * ratio_next / half_width) * residual
            ratio = ratio_next
        correction = correction + direction
        residual = residual - operate(direction.astype(jnp.bfloat16), self_block, hop_blocks)
    return correction, residual
```

```python
import functools

import jax
import jax.numpy as jnp
from jax import lax
from jax.experimental import pallas as pl
from jax.experimental.pallas import tpu as pltpu
from jax.sharding import PartitionSpec as P

MESH = pl.DeviceIdType.MESH
STEPS = 4
CHUNKS = 2
SITES = 16
PLANE = 8
BLOCKS = 8

SHIFT = 1.5
CENTER = 1.5
HALF_WIDTH = 1.0


def coefficients():
    ratio = HALF_WIDTH / CENTER
    pairs = [None]
    for _ in range(1, STEPS):
        following = 1.0 / (2.0 * CENTER / HALF_WIDTH - ratio)
        pairs.append((following * ratio, 2.0 * following / HALF_WIDTH))
        ratio = following
    return pairs


def kernel(
    r_hbm, self_hbm, hop_hbm, corr, res,
    raw_self, raw_hop, weights, v, ht, hx, direction,
    load_sem, v_sem, send_sem, recv_sem,
):
    groups, times = lax.axis_size("group"), lax.axis_size("site")
    g, t = lax.axis_index("group"), lax.axis_index("site")
    g_up, g_down = lax.rem(g + 1, groups), lax.rem(g + groups - 1, groups)
    t_up, t_down = lax.rem(t + 1, times), lax.rem(t + times - 1, times)
    rows = v.shape[3]
    coefs = coefficients()

    first = g * SITES
    load_self = pltpu.make_async_copy(
        self_hbm.at[0, pl.ds(first, SITES)], raw_self, load_sem.at[0]
    )
    load_hop = pltpu.make_async_copy(
        hop_hbm.at[0, pl.ds(first, SITES)], raw_hop, load_sem.at[1]
    )
    load_hop.start()
    load_self.start()

    def load_v(c):
        return pltpu.make_async_copy(
            r_hbm.at[0, :, pl.ds(c * rows, rows)], v.at[0, c], v_sem.at[c]
        )

    for c in range(CHUNKS):
        load_v(c).start()

    def sends(k, c):
        mine = v.at[k, c]
        targets = (
            (mine, ht.at[k, c, 0], (g, t_down)),
            (mine, ht.at[k, c, 1], (g, t_up)),
            (mine.at[pl.ds(0, PLANE)], hx.at[k, c, 0], (g_down, t)),
            (mine.at[pl.ds(PLANE, PLANE)], hx.at[k, c, 1], (g_up, t)),
        )
        return [
            pltpu.make_async_remote_copy(
                src_ref=src,
                dst_ref=dst,
                send_sem=send_sem.at[k, c, i],
                recv_sem=recv_sem.at[k, c, i],
                device_id=device,
                device_id_type=MESH,
            )
            for i, (src, dst, device) in enumerate(targets)
        ]

    barrier = pltpu.get_barrier_semaphore()
    for device in ((g, t_down), (g, t_up), (g_down, t), (g_up, t)):
        pl.semaphore_signal(barrier, inc=1, device_id=device, device_id_type=MESH)
    pl.semaphore_wait(barrier, 4)

    for c in range(CHUNKS):
        load_v(c).wait()
        for copy in sends(0, c):
            copy.start()

    load_self.wait()
    load_hop.wait()
    sign = jnp.where(
        lax.broadcasted_iota(jnp.int32, (64, 128), 1) < 64, 1.0, -1.0
    ).astype(jnp.float32)

    def build(s, carry):
        hop = [raw_hop[s, m].astype(jnp.float32) for m in range(8)]
        blocks = [raw_self[s].astype(jnp.float32), hop[4] + hop[5]]
        blocks += [hop[m] for m in (0, 1, 2, 3, 6, 7)]
        for m, block in enumerate(blocks):
            weights[s, 0:64, m * 128 : (m + 1) * 128] = (block * sign).astype(jnp.bfloat16)
            weights[s, 64:128, m * 128 : (m + 1) * 128] = pltpu.roll(
                block, 64, 1
            ).astype(jnp.bfloat16)
        return carry

    lax.fori_loop(0, SITES, build, 0)

    def compute(k, c):
        def position(p, carry):
            partner = p + 1 - 2 * lax.rem(p, 2)
            y_up, y_down = lax.rem(p + 2, PLANE), lax.rem(p + 6, PLANE)
            for x in range(2):
                base = x * PLANE
                s = base + p
                own = v[k, c, s]
                x_up = v[k, c, PLANE + p] if x == 0 else hx[k, c, 0, p]
                x_down = hx[k, c, 1, p] if x == 0 else v[k, c, p]
                lhs = jnp.concatenate(
                    [
                        own,
                        v[k, c, base + partner],
                        x_up,
                        x_down,
                        v[k, c, base + y_up],
                        v[k, c, base + y_down],
                        ht[k, c, 0, s],
                        ht[k, c, 1, s],
                    ],
                    axis=-1,
                )
                mixed = lax.dot_general(
                    lhs,
                    weights[s],
                    (((1,), (1,)), ((), ())),
                    preferred_element_type=jnp.float32,
                )
                here = pl.ds(c * rows, rows)
                wide = own.astype(jnp.float32)
                if k == 0:
                    residual = mixed * (-1.0 / CENTER)
                    before = wide * (1.0 / CENTER)
                    total = before
                else:
                    residual = res[0, s, here, :] - SHIFT * wide - mixed
                    if k < STEPS - 1:
                        before = direction[c, s]
                        total = corr[0, s, here, :]
                res[0, s, here, :] = residual
                if k < STEPS - 1:
                    scale, gain = coefs[k + 1]
                    now = scale * before + gain * residual
                    direction[c, s] = now
                    corr[0, s, here, :] = total + now
                    v[k + 1, c, s] = now.astype(jnp.bfloat16)
            return carry

        lax.fori_loop(0, PLANE, position, 0)

    for k in range(STEPS):
        for c in range(CHUNKS):
            for copy in sends(k, c):
                copy.wait_recv()
            compute(k, c)
            if k < STEPS - 1:
                for copy in sends(k + 1, c):
                    copy.start()
    for k in range(STEPS):
        for c in range(CHUNKS):
            for copy in sends(k, c):
                copy.wait_send()


def body(residual_in, self_block, hop_blocks):
    count = residual_in.shape[2]
    rows = count // CHUNKS
    out = jax.ShapeDtypeStruct(residual_in.shape, jnp.float32)
    any_space = pl.BlockSpec(memory_space=pl.ANY)
    vmem = pl.BlockSpec(memory_space=pltpu.VMEM)
    return pl.pallas_call(
        kernel,
        out_shape=(out, out),
        in_specs=[any_space] * 3,
        out_specs=(vmem, vmem),
        scratch_shapes=[
            pltpu.VMEM((SITES, 64, 128), jnp.bfloat16),
            pltpu.VMEM((SITES, 8, 64, 128), jnp.bfloat16),
            pltpu.VMEM((SITES, 128, BLOCKS * 128), jnp.bfloat16),
            pltpu.VMEM((STEPS, CHUNKS, SITES, rows, 128), jnp.bfloat16),
            pltpu.VMEM((STEPS, CHUNKS, 2, SITES, rows, 128), jnp.bfloat16),
            pltpu.VMEM((STEPS, CHUNKS, 2, PLANE, rows, 128), jnp.bfloat16),
            pltpu.VMEM((CHUNKS, SITES, rows, 128), jnp.float32),
            pltpu.SemaphoreType.DMA((2,)),
            pltpu.SemaphoreType.DMA((CHUNKS,)),
            pltpu.SemaphoreType.DMA((STEPS, CHUNKS, 4)),
            pltpu.SemaphoreType.DMA((STEPS, CHUNKS, 4)),
        ],
        compiler_params=pltpu.CompilerParams(
            collective_id=0,
            has_side_effects=True,
            vmem_limit_bytes=48 * 1024 * 1024,
        ),
        name="smoother",
    )(residual_in, self_block, hop_blocks)


def solution(mesh):
    return jax.shard_map(
        body,
        mesh=mesh,
        in_specs=(
            P("site", "group", None, None),
            P("site", None, None, None),
            P("site", None, None, None, None),
        ),
        out_specs=(P("site", "group", None, None), P("site", "group", None, None)),
        check_vma=False,
    )
```

```python
import functools

import jax
import jax.numpy as jnp
from jax import lax
from jax.experimental import pallas as pl
from jax.experimental.pallas import tpu as pltpu
from jax.sharding import PartitionSpec as P

MESH = pl.DeviceIdType.MESH
STEPS = 4
SITES = 16
PLANE = 8
BLOCKS = 8
SIZE = 2
GROUPS = SITES // SIZE
WRAP = 16
RELAY = True

SHIFT = 1.5
CENTER = 1.5
HALF_WIDTH = 1.0


def coefficients():
    ratio = HALF_WIDTH / CENTER
    pairs = [None]
    for _ in range(1, STEPS):
        following = 1.0 / (2.0 * CENTER / HALF_WIDTH - ratio)
        pairs.append((following * ratio, 2.0 * following / HALF_WIDTH))
        ratio = following
    return pairs


def relayed(j):
    return RELAY and j % 2 == 1


def kernel(
    r_hbm, self_hbm, hop_hbm, corr, res,
    raw_self, raw_hop, weights, v, ht, hx, passing, direction,
    load_sem, send_sem, recv_sem, pass_sem, forward_sem,
):
    groups, times = lax.axis_size("group"), lax.axis_size("site")
    g, t = lax.axis_index("group"), lax.axis_index("site")
    odd = lax.rem(g, 2)
    other_chip = lax.rem(g + groups - 1 + 2 * odd, groups)
    other_core = g + 1 - 2 * odd
    t_up, t_down = lax.rem(t + 1, times), lax.rem(t + times - 1, times)
    place = lax.rem(t, WRAP)
    coefs = coefficients()
    base = (odd * PLANE, PLANE - odd * PLANE)

    def loads():
        copies = []
        for role in range(2):
            here, there = pl.ds(role * PLANE, PLANE), pl.ds(base[role], PLANE)
            far = pl.ds(g * SITES + base[role], PLANE)
            copies += [
                (hop_hbm.at[0, far], raw_hop.at[here]),
                (self_hbm.at[0, far], raw_self.at[here]),
                (r_hbm.at[0, there], v.at[0, here]),
            ]
        return [
            pltpu.make_async_copy(src, dst, load_sem.at[i])
            for i, (src, dst) in enumerate(copies)
        ]

    for copy in loads():
        copy.start()

    def remote(src, dst, send, recv, device):
        return pltpu.make_async_remote_copy(
            src_ref=src,
            dst_ref=dst,
            send_sem=send,
            recv_sem=recv,
            device_id=device,
            device_id_type=MESH,
        )

    def faces(k, j):
        role, inside = divmod(j, GROUPS // 2)
        here = pl.ds(j * SIZE, SIZE)
        if k == 0:
            mine = r_hbm.at[0, pl.ds(base[role] + inside * SIZE, SIZE)]
        else:
            mine = v.at[k, here]
        partner = other_core if role else other_chip
        landing = hx.at[k, role, pl.ds(inside * SIZE, SIZE)]
        targets = (
            (ht.at[k, 0, here], (g, t_down)),
            (ht.at[k, 1, here], (g, t_up)),
            (landing, (partner, t)),
        )
        return [
            remote(mine, dst, send_sem.at[k, j, i], recv_sem.at[k, j, i], device)
            for i, (dst, device) in enumerate(targets)
        ], mine

    def send(k, j):
        copies, mine = faces(k, j)
        if relayed(j):
            for i, edge, step in ((0, 0, 3), (1, WRAP - 1, -3)):
                detour = remote(
                    mine,
                    passing.at[k, j // 2],
                    send_sem.at[k, j, i],
                    pass_sem.at[k, j // 2],
                    (g, t + step),
                )

                @pl.when(place == edge)
                def _(detour=detour):
                    detour.start()

                @pl.when(place != edge)
                def _(direct=copies[i]):
                    direct.start()

        else:
            copies[0].start()
            copies[1].start()
        copies[2].start()

    def forwards(k, j):
        here = pl.ds(j * SIZE, SIZE)
        out = []
        for i, spot, step in ((0, 3, times - 4), (1, WRAP - 4, 4)):
            out.append((
                spot,
                remote(
                    passing.at[k, j // 2],
                    ht.at[k, i, here],
                    forward_sem.at[k, j // 2],
                    recv_sem.at[k, j, i],
                    (g, lax.rem(t + step, times)),
                ),
                remote(
                    passing.at[k, j // 2],
                    passing.at[k, j // 2],
                    forward_sem.at[k, j // 2],
                    pass_sem.at[k, j // 2],
                    (g, t_up),
                ),
            ))
        return out

    def forward(k, j):
        if relayed(j):
            for spot, onward, arrival in forwards(k, j):

                @pl.when(place == spot)
                def _(onward=onward, arrival=arrival):
                    arrival.wait_recv()
                    onward.start()

    barrier = pltpu.get_barrier_semaphore()

    def greet(device):
        pl.semaphore_signal(barrier, inc=1, device_id=device, device_id_type=MESH)

    for device in ((g, t_down), (g, t_up), (other_chip, t), (other_core, t)):
        greet(device)
    guests = 4
    if RELAY:
        greetings = (
            (0, lax.rem(t + times - 4, times)),
            (WRAP - 1, lax.rem(t + 4, times)),
            (3, t - 3),
            (WRAP - 4, t + 3),
        )
        for spot, device in greetings:
            guests += jnp.where(place == spot, 1, 0)

            @pl.when(place == spot)
            def _(device=device):
                greet((g, device))

    pl.semaphore_wait(barrier, guests)

    for j in range(GROUPS):
        send(0, j)
    for copy in loads():
        copy.wait()

    sign = jnp.where(
        lax.broadcasted_iota(jnp.int32, (64, 128), 1) < 64, 1.0, -1.0
    ).astype(jnp.float32)

    def build(role):
        plane = odd if role == 0 else 1 - odd

        def one(p, carry):
            s = role * PLANE + p

            def hop(m):
                return raw_hop[s, m].astype(jnp.float32)

            blocks = [
                raw_self[s].astype(jnp.float32),
                hop(4) + hop(5),
                hop(plane),
                hop(1 - plane),
                hop(2),
                hop(3),
                hop(6),
                hop(7),
            ]
            for m, block in enumerate(blocks):
                full = jnp.concatenate([block * sign, pltpu.roll(block, 64, 1)], axis=0)
                weights[s, m * 128 : (m + 1) * 128, :] = full.T.astype(jnp.bfloat16)
            return carry

        lax.fori_loop(0, PLANE, one, 0)

    build(0)
    build(1)

    def compute(k, j):
        role, inside = divmod(j, GROUPS // 2)

        def one(p):
            s = role * PLANE + p
            partner = p + 1 if p % 2 == 0 else p - 1
            own = v[k, s]
            lhs = jnp.concatenate(
                [
                    own,
                    v[k, role * PLANE + partner],
                    v[k, (1 - role) * PLANE + p],
                    hx[k, role, p],
                    v[k, role * PLANE + (p + 2) % PLANE],
                    v[k, role * PLANE + (p + 6) % PLANE],
                    ht[k, 0, s],
                    ht[k, 1, s],
                ],
                axis=-1,
            )
            mixed = jnp.dot(lhs, weights[s], preferred_element_type=jnp.float32)
            out = base[role] + p
            wide = own.astype(jnp.float32)
            if k == 0:
                residual = mixed * (-1.0 / CENTER)
                before = wide * (1.0 / CENTER)
                total = before
            else:
                residual = res[0, out] - SHIFT * wide - mixed
                if k < STEPS - 1:
                    before = direction[s]
                    total = corr[0, out]
            res[0, out] = residual
            if k < STEPS - 1:
                scale, gain = coefs[k + 1]
                now = scale * before + gain * residual
                direction[s] = now
                corr[0, out] = total + now
                v[k + 1, s] = now.astype(jnp.bfloat16)

        for p in range(inside * SIZE, (inside + 1) * SIZE):
            one(p)

    for k in range(STEPS):
        for j in range(GROUPS):
            for copy in faces(k, j)[0]:
                copy.wait_recv()
            forward(k, j)
            compute(k, j)
            if k < STEPS - 1:
                send(k + 1, j)
    for k in range(STEPS):
        for j in range(GROUPS):
            for copy in faces(k, j)[0]:
                copy.wait_send()
            if relayed(j):
                for spot, onward, _ in forwards(k, j):

                    @pl.when(place == spot)
                    def _(onward=onward):
                        onward.wait_send()


def store(corr_in, res_in, corr_out, res_out, sems):
    parts = 4
    size = SITES // parts
    copies = []
    for a, (src, dst) in enumerate(((corr_in, corr_out), (res_in, res_out))):
        for i in range(parts):
            here = pl.ds(i * size, size)
            copies.append(
                pltpu.make_async_copy(src.at[0, here], dst.at[0, here], sems.at[a, i])
            )
    for copy in copies:
        copy.start()
    for copy in copies:
        copy.wait()


def body(residual_in, self_block, hop_blocks):
    out = jax.ShapeDtypeStruct(residual_in.shape, jnp.float32)
    hbm = pl.BlockSpec(memory_space=pltpu.HBM)
    vmem = pl.BlockSpec(memory_space=pltpu.VMEM)
    tile = (128, 128)
    results = pl.pallas_call(
        kernel,
        out_shape=(out, out),
        in_specs=[hbm] * 3,
        out_specs=(vmem, vmem),
        scratch_shapes=[
            pltpu.VMEM((SITES, 64, 128), jnp.bfloat16),
            pltpu.VMEM((SITES, 8, 64, 128), jnp.bfloat16),
            pltpu.VMEM((SITES, BLOCKS * 128, 128), jnp.bfloat16),
            pltpu.VMEM((STEPS, SITES) + tile, jnp.bfloat16),
            pltpu.VMEM((STEPS, 2, SITES) + tile, jnp.bfloat16),
            pltpu.VMEM((STEPS, 2, PLANE) + tile, jnp.bfloat16),
            pltpu.VMEM((STEPS, GROUPS // 2, SIZE) + tile, jnp.bfloat16),
            pltpu.VMEM((SITES,) + tile, jnp.float32),
            pltpu.SemaphoreType.DMA((6,)),
            pltpu.SemaphoreType.DMA((STEPS, GROUPS, 3)),
            pltpu.SemaphoreType.DMA((STEPS, GROUPS, 3)),
            pltpu.SemaphoreType.DMA((STEPS, GROUPS // 2)),
            pltpu.SemaphoreType.DMA((STEPS, GROUPS // 2)),
        ],
        compiler_params=pltpu.CompilerParams(
            collective_id=0,
            has_side_effects=True,
            vmem_limit_bytes=48 * 1024 * 1024,
        ),
        name="smoother",
    )(*(pltpu.with_memory_space_constraint(x, pltpu.HBM) for x in (residual_in, self_block, hop_blocks)))
    return pl.pallas_call(
        store,
        out_shape=(out, out),
        in_specs=[pl.BlockSpec(memory_space=pl.ANY)] * 2,
        out_specs=(hbm, hbm),
        scratch_shapes=[pltpu.SemaphoreType.DMA((2, 4))],
        name="store",
    )(*(pltpu.with_memory_space_constraint(x, pltpu.VMEM) for x in results))


def solution(mesh):
    return jax.shard_map(
        body,
        mesh=mesh,
        in_specs=(
            P("site", "group", None, None),
            P("site", None, None, None),
            P("site", None, None, None, None),
        ),
        out_specs=(P("site", "group", None, None), P("site", "group", None, None)),
        check_vma=False,
    )
```

```python
import functools

import jax
import jax.numpy as jnp
from jax import lax
from jax.experimental import pallas as pl
from jax.experimental.pallas import tpu as pltpu
from jax.sharding import PartitionSpec as P

MESH = pl.DeviceIdType.MESH
STEPS = 4
SITES = 16
PLANE = 8
BLOCKS = 8
SIZE = 2
GROUPS = SITES // SIZE
WRAP = 16
RELAY = True

SHIFT = 1.5
CENTER = 1.5
HALF_WIDTH = 1.0


def coefficients():
    ratio = HALF_WIDTH / CENTER
    pairs = [None]
    for _ in range(1, STEPS):
        following = 1.0 / (2.0 * CENTER / HALF_WIDTH - ratio)
        pairs.append((following * ratio, 2.0 * following / HALF_WIDTH))
        ratio = following
    return pairs


ORDERS = ((0, 2, 1, 4, 3, 6, 5, 7), (1, 0, 3, 2, 5, 4, 7, 6))


def relayed(k, j):
    return RELAY and (j + k) % 2 == 1


def kernel(
    r_hbm, self_hbm, hop_hbm, corr, res,
    raw_self, raw_hop, weights, v, ht, hx, passing, direction,
    load_sem, send_sem, recv_sem, pass_sem, forward_sem,
):
    groups, times = lax.axis_size("group"), lax.axis_size("site")
    g, t = lax.axis_index("group"), lax.axis_index("site")
    odd = lax.rem(g, 2)
    other_chip = lax.rem(g + groups - 1 + 2 * odd, groups)
    other_core = g + 1 - 2 * odd
    t_up, t_down = lax.rem(t + 1, times), lax.rem(t + times - 1, times)
    place = lax.rem(t, WRAP)
    coefs = coefficients()
    base = (odd * PLANE, PLANE - odd * PLANE)

    def loads():
        copies = []
        for role in range(2):
            here, there = pl.ds(role * PLANE, PLANE), pl.ds(base[role], PLANE)
            far = pl.ds(g * SITES + base[role], PLANE)
            copies += [
                (hop_hbm.at[0, far], raw_hop.at[here]),
                (self_hbm.at[0, far], raw_self.at[here]),
                (r_hbm.at[0, there], v.at[0, here]),
            ]
        return [
            pltpu.make_async_copy(src, dst, load_sem.at[i % 3])
            for i, (src, dst) in enumerate(copies)
        ]

    for copy in loads():
        copy.start()

    def remote(src, dst, send, recv, device):
        return pltpu.make_async_remote_copy(
            src_ref=src,
            dst_ref=dst,
            send_sem=send,
            recv_sem=recv,
            device_id=device,
            device_id_type=MESH,
        )

    def faces(k, j):
        role, inside = divmod(j, GROUPS // 2)
        here = pl.ds(j * SIZE, SIZE)
        if k == 0:
            mine = r_hbm.at[0, pl.ds(base[role] + inside * SIZE, SIZE)]
        else:
            mine = v.at[k, here]
        partner = other_core if role else other_chip
        landing = hx.at[k, role, pl.ds(inside * SIZE, SIZE)]
        targets = (
            (ht.at[k, 0, here], (g, t_down)),
            (ht.at[k, 1, here], (g, t_up)),
            (landing, (partner, t)),
        )
        return [
            remote(mine, dst, send_sem.at[k, i // 2], recv_sem.at[k, j], device)
            for i, (dst, device) in enumerate(targets)
        ], mine

    def send(k, j):
        copies, mine = faces(k, j)
        if relayed(k, j):
            for i, edge, step in ((0, 0, 3), (1, WRAP - 1, -3)):
                detour = remote(
                    mine,
                    passing.at[k, j // 2],
                    send_sem.at[k, 0],
                    pass_sem.at[k, j // 2],
                    (g, t + step),
                )

                @pl.when(place == edge)
                def _(detour=detour):
                    detour.start()

                @pl.when(place != edge)
                def _(direct=copies[i]):
                    direct.start()

        else:
            copies[0].start()
            copies[1].start()
        copies[2].start()

    def forwards(k, j):
        here = pl.ds(j * SIZE, SIZE)
        out = []
        for i, spot, step in ((0, 3, times - 4), (1, WRAP - 4, 4)):
            out.append((
                spot,
                remote(
                    passing.at[k, j // 2],
                    ht.at[k, i, here],
                    forward_sem.at[k],
                    recv_sem.at[k, j],
                    (g, lax.rem(t + step, times)),
                ),
                remote(
                    passing.at[k, j // 2],
                    passing.at[k, j // 2],
                    forward_sem.at[k],
                    pass_sem.at[k, j // 2],
                    (g, t_up),
                ),
            ))
        return out

    def forward(k, j):
        if relayed(k, j):
            for spot, onward, arrival in forwards(k, j):

                @pl.when(place == spot)
                def _(onward=onward, arrival=arrival):
                    arrival.wait_recv()
                    onward.start()

    barrier = pltpu.get_barrier_semaphore()

    def greet(device):
        pl.semaphore_signal(barrier, inc=1, device_id=device, device_id_type=MESH)

    for device in ((g, t_down), (g, t_up), (other_chip, t), (other_core, t)):
        greet(device)
    guests = 4
    if RELAY:
        greetings = (
            (0, lax.rem(t + times - 4, times)),
            (WRAP - 1, lax.rem(t + 4, times)),
            (3, t - 3),
            (WRAP - 4, t + 3),
        )
        for spot, device in greetings:
            guests += jnp.where(place == spot, 1, 0)

            @pl.when(place == spot)
            def _(device=device):
                greet((g, device))

    pl.semaphore_wait(barrier, guests)

    for j in ORDERS[1]:
        send(0, j)
    whole = (
        (hop_hbm.at[0, pl.ds(0, SITES)], raw_hop),
        (self_hbm.at[0, pl.ds(0, SITES)], raw_self),
        (r_hbm.at[0], v.at[0]),
    )
    for i, (src, dst) in enumerate(whole):
        pltpu.make_async_copy(src, dst, load_sem.at[i]).wait()

    sign = jnp.where(
        lax.broadcasted_iota(jnp.int32, (64, 128), 1) < 64, 1.0, -1.0
    ).astype(jnp.float32)

    def build(role):
        plane = odd if role == 0 else 1 - odd

        def one(p, carry):
            s = role * PLANE + p

            def hop(m):
                return raw_hop[s, m].astype(jnp.float32)

            blocks = [
                raw_self[s].astype(jnp.float32),
                hop(4) + hop(5),
                hop(plane),
                hop(1 - plane),
                hop(2),
                hop(3),
                hop(6),
                hop(7),
            ]
            for m, block in enumerate(blocks):
                full = jnp.concatenate([block * sign, pltpu.roll(block, 64, 1)], axis=0)
                weights[s, m * 128 : (m + 1) * 128, :] = full.T.astype(jnp.bfloat16)
            return carry

        lax.fori_loop(0, PLANE, one, 0)

    build(0)
    build(1)

    def compute(k, j):
        role, inside = divmod(j, GROUPS // 2)

        def one(p):
            s = role * PLANE + p
            partner = p + 1 if p % 2 == 0 else p - 1
            own = v[k, s]
            lhs = jnp.concatenate(
                [
                    own,
                    v[k, role * PLANE + partner],
                    v[k, (1 - role) * PLANE + p],
                    hx[k, role, p],
                    v[k, role * PLANE + (p + 2) % PLANE],
                    v[k, role * PLANE + (p + 6) % PLANE],
                    ht[k, 0, s],
                    ht[k, 1, s],
                ],
                axis=-1,
            )
            mixed = jnp.dot(lhs, weights[s], preferred_element_type=jnp.float32)
            out = base[role] + p
            wide = own.astype(jnp.float32)
            if k == 0:
                residual = mixed * (-1.0 / CENTER)
                before = wide * (1.0 / CENTER)
                total = before
            else:
                residual = res[0, out] - SHIFT * wide - mixed
                if k < STEPS - 1:
                    before = direction[s]
                    total = corr[0, out]
            res[0, out] = residual
            if k < STEPS - 1:
                scale, gain = coefs[k + 1]
                now = scale * before + gain * residual
                direction[s] = now
                corr[0, out] = total + now
                v[k + 1, s] = now.astype(jnp.bfloat16)

        for p in range(inside * SIZE, (inside + 1) * SIZE):
            one(p)

    def all_bytes(ref, send, recv):
        return remote(ref, ref, send, recv, (g, t_up))

    for k in range(STEPS):
        waiting = [j for j in range(GROUPS) if relayed(k, j)]
        for place_in_step, j in enumerate(ORDERS[k % 2]):
            if place_in_step % 2 == 0 and waiting:
                forward(k, waiting.pop(0))
            three = v.at[k, pl.ds(0, 3 * SIZE)]
            all_bytes(three, send_sem.at[k, 0], recv_sem.at[k, j]).wait_recv()
            compute(k, j)
            if k < STEPS - 1:
                send(k + 1, j)
    for k in range(STEPS):
        all_bytes(ht.at[k], send_sem.at[k, 0], recv_sem.at[k, 0]).wait_send()
        all_bytes(v.at[k], send_sem.at[k, 1], recv_sem.at[k, 0]).wait_send()
    if RELAY:

        @pl.when((place == 3) | (place == WRAP - 4))
        def _():
            for k in range(STEPS):
                half = v.at[k, pl.ds(0, SITES // 2)]
                all_bytes(half, forward_sem.at[k], recv_sem.at[k, 0]).wait_send()


def store(corr_in, res_in, corr_out, res_out, sems):
    parts = 4
    size = SITES // parts
    copies = []
    for a, (src, dst) in enumerate(((corr_in, corr_out), (res_in, res_out))):
        for i in range(parts):
            here = pl.ds(i * size, size)
            copies.append(
                pltpu.make_async_copy(src.at[0, here], dst.at[0, here], sems.at[a, i])
            )
    for copy in copies:
        copy.start()
    for copy in copies:
        copy.wait()


def body(residual_in, self_block, hop_blocks):
    out = jax.ShapeDtypeStruct(residual_in.shape, jnp.float32)
    hbm = pl.BlockSpec(memory_space=pltpu.HBM)
    vmem = pl.BlockSpec(memory_space=pltpu.VMEM)
    tile = (128, 128)
    results = pl.pallas_call(
        kernel,
        out_shape=(out, out),
        in_specs=[hbm] * 3,
        out_specs=(vmem, vmem),
        scratch_shapes=[
            pltpu.VMEM((SITES, 64, 128), jnp.bfloat16),
            pltpu.VMEM((SITES, 8, 64, 128), jnp.bfloat16),
            pltpu.VMEM((SITES, BLOCKS * 128, 128), jnp.bfloat16),
            pltpu.VMEM((STEPS, SITES) + tile, jnp.bfloat16),
            pltpu.VMEM((STEPS, 2, SITES) + tile, jnp.bfloat16),
            pltpu.VMEM((STEPS, 2, PLANE) + tile, jnp.bfloat16),
            pltpu.VMEM((STEPS, GROUPS // 2, SIZE) + tile, jnp.bfloat16),
            pltpu.VMEM((SITES,) + tile, jnp.float32),
            pltpu.SemaphoreType.DMA((3,)),
            pltpu.SemaphoreType.DMA((STEPS, 2)),
            pltpu.SemaphoreType.DMA((STEPS, GROUPS)),
            pltpu.SemaphoreType.DMA((STEPS, GROUPS // 2)),
            pltpu.SemaphoreType.DMA((STEPS,)),
        ],
        compiler_params=pltpu.CompilerParams(
            collective_id=0,
            has_side_effects=True,
            vmem_limit_bytes=48 * 1024 * 1024,
        ),
        name="smoother",
    )(*(pltpu.with_memory_space_constraint(x, pltpu.HBM) for x in (residual_in, self_block, hop_blocks)))
    return pl.pallas_call(
        store,
        out_shape=(out, out),
        in_specs=[pl.BlockSpec(memory_space=pl.ANY)] * 2,
        out_specs=(hbm, hbm),
        scratch_shapes=[pltpu.SemaphoreType.DMA((2, 4))],
        name="store",
    )(*(pltpu.with_memory_space_constraint(x, pltpu.VMEM) for x in results))


def solution(mesh):
    return jax.shard_map(
        body,
        mesh=mesh,
        in_specs=(
            P("site", "group", None, None),
            P("site", None, None, None),
            P("site", None, None, None, None),
        ),
        out_specs=(P("site", "group", None, None), P("site", "group", None, None)),
        check_vma=False,
    )
```

```python
import functools

import jax
import jax.numpy as jnp
from jax import lax
from jax.experimental import pallas as pl
from jax.experimental.pallas import tpu as pltpu
from jax.sharding import PartitionSpec as P

MESH = pl.DeviceIdType.MESH
STEPS = 4
SITES = 16
PLANE = 8
BLOCKS = 8
SIZE = 2
GROUPS = SITES // SIZE
WRAP = 16
RELAY = True

SHIFT = 1.5
CENTER = 1.5
HALF_WIDTH = 1.0


def coefficients():
    ratio = HALF_WIDTH / CENTER
    pairs = [None]
    for _ in range(1, STEPS):
        following = 1.0 / (2.0 * CENTER / HALF_WIDTH - ratio)
        pairs.append((following * ratio, 2.0 * following / HALF_WIDTH))
        ratio = following
    return pairs


ORDERS = ((0, 2, 1, 4, 3, 6, 5, 7), (1, 0, 3, 2, 5, 4, 7, 6))


def relayed(k, j):
    return RELAY and (j + k) % 2 == 1


def kernel(
    r_hbm, self_hbm, hop_hbm, corr, res,
    raw_self, raw_hop, weights, v, ht, hx, passing, direction,
    load_sem, send_sem, recv_sem, pass_sem, forward_sem,
):
    groups, times = lax.axis_size("group"), lax.axis_size("site")
    g, t = lax.axis_index("group"), lax.axis_index("site")
    odd = lax.rem(g, 2)
    other_chip = lax.rem(g + groups - 1 + 2 * odd, groups)
    other_core = g + 1 - 2 * odd
    t_up, t_down = lax.rem(t + 1, times), lax.rem(t + times - 1, times)
    place = lax.rem(t, WRAP)
    coefs = coefficients()
    base = (odd * PLANE, PLANE - odd * PLANE)

    def loads():
        copies = []
        for role in range(2):
            here, there = pl.ds(role * PLANE, PLANE), pl.ds(base[role], PLANE)
            far = pl.ds(g * SITES + base[role], PLANE)
            copies += [
                (hop_hbm.at[0, far], raw_hop.at[here]),
                (self_hbm.at[0, far], raw_self.at[here]),
                (r_hbm.at[0, there], v.at[0, here]),
            ]
        return [
            pltpu.make_async_copy(src, dst, load_sem.at[i % 3])
            for i, (src, dst) in enumerate(copies)
        ]

    for copy in loads():
        copy.start()

    def remote(src, dst, send, recv, device):
        return pltpu.make_async_remote_copy(
            src_ref=src,
            dst_ref=dst,
            send_sem=send,
            recv_sem=recv,
            device_id=device,
            device_id_type=MESH,
        )

    def faces(k, j):
        role, inside = divmod(j, GROUPS // 2)
        here = pl.ds(j * SIZE, SIZE)
        if k == 0:
            mine = r_hbm.at[0, pl.ds(base[role] + inside * SIZE, SIZE)]
        else:
            mine = v.at[k, here]
        partner = other_core if role else other_chip
        landing = hx.at[k, role, pl.ds(inside * SIZE, SIZE)]
        targets = (
            (ht.at[k, 0, here], (g, t_down)),
            (ht.at[k, 1, here], (g, t_up)),
            (landing, (partner, t)),
        )
        return [
            remote(mine, dst, send_sem.at[k, i // 2], recv_sem.at[k, j], device)
            for i, (dst, device) in enumerate(targets)
        ], mine

    def send(k, j):
        copies, mine = faces(k, j)
        if relayed(k, j):
            for i, edge, step in ((0, 0, 3), (1, WRAP - 1, -3)):
                detour = remote(
                    mine,
                    passing.at[k, j // 2],
                    send_sem.at[k, 0],
                    pass_sem.at[k, j // 2],
                    (g, t + step),
                )

                @pl.when(place == edge)
                def _(detour=detour):
                    detour.start()

                @pl.when(place != edge)
                def _(direct=copies[i]):
                    direct.start()

        else:
            copies[0].start()
            copies[1].start()
        copies[2].start()

    def forwards(k, j):
        here = pl.ds(j * SIZE, SIZE)
        out = []
        for i, spot, step in ((0, 3, times - 4), (1, WRAP - 4, 4)):
            out.append((
                spot,
                remote(
                    passing.at[k, j // 2],
                    ht.at[k, i, here],
                    forward_sem.at[k],
                    recv_sem.at[k, j],
                    (g, lax.rem(t + step, times)),
                ),
                remote(
                    passing.at[k, j // 2],
                    passing.at[k, j // 2],
                    forward_sem.at[k],
                    pass_sem.at[k, j // 2],
                    (g, t_up),
                ),
            ))
        return out

    def forward(k, j):
        if relayed(k, j):
            for spot, onward, arrival in forwards(k, j):

                @pl.when(place == spot)
                def _(onward=onward, arrival=arrival):
                    arrival.wait_recv()
                    onward.start()

    barrier = pltpu.get_barrier_semaphore()

    def greet(device):
        pl.semaphore_signal(barrier, inc=1, device_id=device, device_id_type=MESH)

    for device in ((g, t_down), (g, t_up), (other_chip, t), (other_core, t)):
        greet(device)
    guests = 4
    if RELAY:
        greetings = (
            (0, lax.rem(t + times - 4, times)),
            (WRAP - 1, lax.rem(t + 4, times)),
            (3, t - 3),
            (WRAP - 4, t + 3),
        )
        for spot, device in greetings:
            guests += jnp.where(place == spot, 1, 0)

            @pl.when(place == spot)
            def _(device=device):
                greet((g, device))

    pl.semaphore_wait(barrier, guests)

    for j in ORDERS[1]:
        send(0, j)
    whole = (
        (hop_hbm.at[0, pl.ds(0, SITES)], raw_hop),
        (self_hbm.at[0, pl.ds(0, SITES)], raw_self),
        (r_hbm.at[0], v.at[0]),
    )
    for i, (src, dst) in enumerate(whole):
        pltpu.make_async_copy(src, dst, load_sem.at[i]).wait()

    sign = jnp.where(
        lax.broadcasted_iota(jnp.int32, (64, 128), 1) < 64, 1.0, -1.0
    ).astype(jnp.float32)

    def build(role):
        plane = odd if role == 0 else 1 - odd

        def one(p, carry):
            s = role * PLANE + p

            def hop(m):
                return raw_hop[s, m].astype(jnp.float32)

            blocks = [
                raw_self[s].astype(jnp.float32),
                hop(4) + hop(5),
                hop(plane),
                hop(1 - plane),
                hop(2),
                hop(3),
                hop(6),
                hop(7),
            ]
            for m, block in enumerate(blocks):
                full = jnp.concatenate([block * sign, pltpu.roll(block, 64, 1)], axis=0)
                weights[s, m * 128 : (m + 1) * 128, :] = full.T.astype(jnp.bfloat16)
            return carry

        lax.fori_loop(0, PLANE, one, 0)

    build(0)
    build(1)

    def compute(k, j):
        role, inside = divmod(j, GROUPS // 2)

        def one(p):
            s = role * PLANE + p
            partner = p + 1 if p % 2 == 0 else p - 1
            own = v[k, s]
            lhs = jnp.concatenate(
                [
                    own,
                    v[k, role * PLANE + partner],
                    v[k, (1 - role) * PLANE + p],
                    hx[k, role, p],
                    v[k, role * PLANE + (p + 2) % PLANE],
                    v[k, role * PLANE + (p + 6) % PLANE],
                    ht[k, 0, s],
                    ht[k, 1, s],
                ],
                axis=-1,
            )
            mixed = jnp.dot(lhs, weights[s], preferred_element_type=jnp.float32)
            out = base[role] + p
            wide = own.astype(jnp.float32)
            if k == 0:
                residual = mixed * (-1.0 / CENTER)
                before = wide * (1.0 / CENTER)
                total = before
            else:
                residual = res[0, out] - SHIFT * wide - mixed
                if k < STEPS - 1:
                    before = direction[s]
                    total = corr[0, out]
            res[0, out] = residual
            if k < STEPS - 1:
                scale, gain = coefs[k + 1]
                now = scale * before + gain * residual
                direction[s] = now
                corr[0, out] = total + now
                v[k + 1, s] = now.astype(jnp.bfloat16)

        for p in range(inside * SIZE, (inside + 1) * SIZE):
            one(p)

    def all_bytes(ref, send, recv):
        return remote(ref, ref, send, recv, (g, t_up))

    for k in range(STEPS):
        waiting = [j for j in range(GROUPS) if relayed(k, j)]
        for place_in_step, j in enumerate(ORDERS[k % 2]):
            if waiting:
                forward(k, waiting.pop(0))
            three = v.at[k, pl.ds(0, 3 * SIZE)]
            all_bytes(three, send_sem.at[k, 0], recv_sem.at[k, j]).wait_recv()
            compute(k, j)
            if k < STEPS - 1:
                send(k + 1, j)
    for k in range(STEPS):
        all_bytes(ht.at[k], send_sem.at[k, 0], recv_sem.at[k, 0]).wait_send()
        all_bytes(v.at[k], send_sem.at[k, 1], recv_sem.at[k, 0]).wait_send()
    if RELAY:

        @pl.when((place == 3) | (place == WRAP - 4))
        def _():
            for k in range(STEPS):
                half = v.at[k, pl.ds(0, SITES // 2)]
                all_bytes(half, forward_sem.at[k], recv_sem.at[k, 0]).wait_send()


def store(corr_in, res_in, corr_out, res_out, sems):
    parts = 4
    size = SITES // parts
    copies = []
    for a, (src, dst) in enumerate(((corr_in, corr_out), (res_in, res_out))):
        for i in range(parts):
            here = pl.ds(i * size, size)
            copies.append(
                pltpu.make_async_copy(src.at[0, here], dst.at[0, here], sems.at[a, i])
            )
    for copy in copies:
        copy.start()
    for copy in copies:
        copy.wait()


def body(residual_in, self_block, hop_blocks):
    out = jax.ShapeDtypeStruct(residual_in.shape, jnp.float32)
    hbm = pl.BlockSpec(memory_space=pltpu.HBM)
    vmem = pl.BlockSpec(memory_space=pltpu.VMEM)
    tile = (128, 128)
    results = pl.pallas_call(
        kernel,
        out_shape=(out, out),
        in_specs=[hbm] * 3,
        out_specs=(vmem, vmem),
        scratch_shapes=[
            pltpu.VMEM((SITES, 64, 128), jnp.bfloat16),
            pltpu.VMEM((SITES, 8, 64, 128), jnp.bfloat16),
            pltpu.VMEM((SITES, BLOCKS * 128, 128), jnp.bfloat16),
            pltpu.VMEM((STEPS, SITES) + tile, jnp.bfloat16),
            pltpu.VMEM((STEPS, 2, SITES) + tile, jnp.bfloat16),
            pltpu.VMEM((STEPS, 2, PLANE) + tile, jnp.bfloat16),
            pltpu.VMEM((STEPS, GROUPS // 2, SIZE) + tile, jnp.bfloat16),
            pltpu.VMEM((SITES,) + tile, jnp.float32),
            pltpu.SemaphoreType.DMA((3,)),
            pltpu.SemaphoreType.DMA((STEPS, 2)),
            pltpu.SemaphoreType.DMA((STEPS, GROUPS)),
            pltpu.SemaphoreType.DMA((STEPS, GROUPS // 2)),
            pltpu.SemaphoreType.DMA((STEPS,)),
        ],
        compiler_params=pltpu.CompilerParams(
            collective_id=0,
            has_side_effects=True,
            vmem_limit_bytes=48 * 1024 * 1024,
        ),
        name="smoother",
    )(*(pltpu.with_memory_space_constraint(x, pltpu.HBM) for x in (residual_in, self_block, hop_blocks)))
    return pl.pallas_call(
        store,
        out_shape=(out, out),
        in_specs=[pl.BlockSpec(memory_space=pl.ANY)] * 2,
        out_specs=(hbm, hbm),
        scratch_shapes=[pltpu.SemaphoreType.DMA((2, 4))],
        name="store",
    )(*(pltpu.with_memory_space_constraint(x, pltpu.VMEM) for x in results))


def solution(mesh):
    return jax.shard_map(
        body,
        mesh=mesh,
        in_specs=(
            P("site", "group", None, None),
            P("site", None, None, None),
            P("site", None, None, None, None),
        ),
        out_specs=(P("site", "group", None, None), P("site", "group", None, None)),
        check_vma=False,
    )
```

```python
import functools

import jax
import jax.numpy as jnp
from jax import lax
from jax.experimental import pallas as pl
from jax.experimental.pallas import tpu as pltpu
from jax.sharding import PartitionSpec as P

MESH = pl.DeviceIdType.MESH
STEPS = 4
SITES = 16
PLANE = 8
BLOCKS = 8
SIZE = 2
GROUPS = SITES // SIZE
WRAP = 16
RELAY = True

SHIFT = 1.5
CENTER = 1.5
HALF_WIDTH = 1.0


def coefficients():
    ratio = HALF_WIDTH / CENTER
    pairs = [None]
    for _ in range(1, STEPS):
        following = 1.0 / (2.0 * CENTER / HALF_WIDTH - ratio)
        pairs.append((following * ratio, 2.0 * following / HALF_WIDTH))
        ratio = following
    return pairs


ORDERS = ((0, 2, 1, 4, 3, 6, 5, 7), (1, 0, 3, 2, 5, 4, 7, 6))


def relayed(k, j):
    return RELAY and (j + k) % 2 == 1


def kernel(
    r_hbm, self_hbm, hop_hbm, corr, res,
    raw_self, raw_hop, weights, v, ht, hx, passing, direction,
    load_sem, send_sem, recv_sem, pass_sem, forward_sem,
):
    groups, times = lax.axis_size("group"), lax.axis_size("site")
    g, t = lax.axis_index("group"), lax.axis_index("site")
    odd = lax.rem(g, 2)
    other_chip = lax.rem(g + groups - 1 + 2 * odd, groups)
    other_core = g + 1 - 2 * odd
    t_up, t_down = lax.rem(t + 1, times), lax.rem(t + times - 1, times)
    place = lax.rem(t, WRAP)
    coefs = coefficients()
    base = (odd * PLANE, PLANE - odd * PLANE)

    def loads():
        copies = []
        for role in range(2):
            here, there = pl.ds(role * PLANE, PLANE), pl.ds(base[role], PLANE)
            far = pl.ds(g * SITES + base[role], PLANE)
            copies += [
                (hop_hbm.at[0, far], raw_hop.at[here]),
                (self_hbm.at[0, far], raw_self.at[here]),
                (r_hbm.at[0, there], v.at[0, here]),
            ]
        return [
            pltpu.make_async_copy(src, dst, load_sem.at[i % 3])
            for i, (src, dst) in enumerate(copies)
        ]

    for copy in loads():
        copy.start()

    def remote(src, dst, send, recv, device):
        return pltpu.make_async_remote_copy(
            src_ref=src,
            dst_ref=dst,
            send_sem=send,
            recv_sem=recv,
            device_id=device,
            device_id_type=MESH,
        )

    def faces(k, j):
        role, inside = divmod(j, GROUPS // 2)
        here = pl.ds(j * SIZE, SIZE)
        if k == 0:
            mine = r_hbm.at[0, pl.ds(base[role] + inside * SIZE, SIZE)]
        else:
            mine = v.at[k, here]
        partner = other_core if role else other_chip
        landing = hx.at[k, role, pl.ds(inside * SIZE, SIZE)]
        targets = (
            (ht.at[k, 0, here], (g, t_down)),
            (ht.at[k, 1, here], (g, t_up)),
            (landing, (partner, t)),
        )
        return [
            remote(mine, dst, send_sem.at[k, i // 2], recv_sem.at[k, j], device)
            for i, (dst, device) in enumerate(targets)
        ], mine

    def send(k, j):
        copies, mine = faces(k, j)
        if relayed(k, j):
            for i, edge, step in ((0, 0, 3), (1, WRAP - 1, -3)):
                detour = remote(
                    mine,
                    passing.at[k, j // 2],
                    send_sem.at[k, 0],
                    pass_sem.at[k, j // 2],
                    (g, t + step),
                )

                @pl.when(place == edge)
                def _(detour=detour):
                    detour.start()

                @pl.when(place != edge)
                def _(direct=copies[i]):
                    direct.start()

        else:
            copies[0].start()
            copies[1].start()
        copies[2].start()

    def forwards(k, j):
        here = pl.ds(j * SIZE, SIZE)
        out = []
        for i, spot, step in ((0, 3, times - 4), (1, WRAP - 4, 4)):
            out.append((
                spot,
                remote(
                    passing.at[k, j // 2],
                    ht.at[k, i, here],
                    forward_sem.at[k],
                    recv_sem.at[k, j],
                    (g, lax.rem(t + step, times)),
                ),
                remote(
                    passing.at[k, j // 2],
                    passing.at[k, j // 2],
                    forward_sem.at[k],
                    pass_sem.at[k, j // 2],
                    (g, t_up),
                ),
            ))
        return out

    def forward(k, j):
        if relayed(k, j):
            for spot, onward, arrival in forwards(k, j):

                @pl.when(place == spot)
                def _(onward=onward, arrival=arrival):
                    arrival.wait_recv()
                    onward.start()

    barrier = pltpu.get_barrier_semaphore()

    def greet(device):
        pl.semaphore_signal(barrier, inc=1, device_id=device, device_id_type=MESH)

    for device in ((g, t_down), (g, t_up), (other_chip, t), (other_core, t)):
        greet(device)
    guests = 4
    if RELAY:
        greetings = (
            (0, lax.rem(t + times - 4, times)),
            (WRAP - 1, lax.rem(t + 4, times)),
            (3, t - 3),
            (WRAP - 4, t + 3),
        )
        for spot, device in greetings:
            guests += jnp.where(place == spot, 1, 0)

            @pl.when(place == spot)
            def _(device=device):
                greet((g, device))

    pl.semaphore_wait(barrier, guests)

    for j in ORDERS[1]:
        send(0, j)
    whole = (
        (hop_hbm.at[0, pl.ds(0, SITES)], raw_hop),
        (self_hbm.at[0, pl.ds(0, SITES)], raw_self),
        (r_hbm.at[0], v.at[0]),
    )
    for i, (src, dst) in enumerate(whole):
        pltpu.make_async_copy(src, dst, load_sem.at[i]).wait()

    sign = jnp.where(
        lax.broadcasted_iota(jnp.int32, (64, 128), 1) < 64, 1.0, -1.0
    ).astype(jnp.float32)

    def build(role):
        plane = odd if role == 0 else 1 - odd

        def one(p, carry):
            s = role * PLANE + p

            def hop(m):
                return raw_hop[s, m].astype(jnp.float32)

            blocks = [
                raw_self[s].astype(jnp.float32),
                hop(4) + hop(5),
                hop(plane),
                hop(1 - plane),
                hop(2),
                hop(3),
                hop(6),
                hop(7),
            ]
            for m, block in enumerate(blocks):
                full = jnp.concatenate([block * sign, pltpu.roll(block, 64, 1)], axis=0)
                weights[s, m * 128 : (m + 1) * 128, :] = full.T.astype(jnp.bfloat16)
            return carry

        lax.fori_loop(0, PLANE, one, 0)

    build(0)
    build(1)

    def compute(k, j):
        role, inside = divmod(j, GROUPS // 2)

        def one(p):
            s = role * PLANE + p
            partner = p + 1 if p % 2 == 0 else p - 1
            own = v[k, s]
            lhs = jnp.concatenate(
                [
                    own,
                    v[k, role * PLANE + partner],
                    v[k, (1 - role) * PLANE + p],
                    hx[k, role, p],
                    v[k, role * PLANE + (p + 2) % PLANE],
                    v[k, role * PLANE + (p + 6) % PLANE],
                    ht[k, 0, s],
                    ht[k, 1, s],
                ],
                axis=-1,
            )
            mixed = jnp.dot(lhs, weights[s], preferred_element_type=jnp.float32)
            out = base[role] + p
            wide = own.astype(jnp.float32)
            if k == 0:
                residual = mixed * (-1.0 / CENTER)
                before = wide * (1.0 / CENTER)
                total = before
            else:
                residual = res[0, out] - SHIFT * wide - mixed
                if k < STEPS - 1:
                    before = direction[s]
                    total = corr[0, out]
            res[0, out] = residual
            if k < STEPS - 1:
                scale, gain = coefs[k + 1]
                now = scale * before + gain * residual
                direction[s] = now
                corr[0, out] = total + now
                v[k + 1, s] = now.astype(jnp.bfloat16)

        for p in range(inside * SIZE, (inside + 1) * SIZE):
            one(p)

    def all_bytes(ref, send, recv):
        return remote(ref, ref, send, recv, (g, t_up))

    for k in range(STEPS):
        waiting = [j for j in range(GROUPS) if relayed(k, j)]
        for place_in_step, j in enumerate(ORDERS[k % 2]):
            for _ in waiting[:2]:
                forward(k, waiting.pop(0))
            three = v.at[k, pl.ds(0, 3 * SIZE)]
            all_bytes(three, send_sem.at[k, 0], recv_sem.at[k, j]).wait_recv()
            compute(k, j)
            if k < STEPS - 1:
                send(k + 1, j)
    for k in range(STEPS):
        all_bytes(ht.at[k], send_sem.at[k, 0], recv_sem.at[k, 0]).wait_send()
        all_bytes(v.at[k], send_sem.at[k, 1], recv_sem.at[k, 0]).wait_send()
    if RELAY:

        @pl.when((place == 3) | (place == WRAP - 4))
        def _():
            for k in range(STEPS):
                half = v.at[k, pl.ds(0, SITES // 2)]
                all_bytes(half, forward_sem.at[k], recv_sem.at[k, 0]).wait_send()


def store(corr_in, res_in, corr_out, res_out, sems):
    parts = 4
    size = SITES // parts
    copies = []
    for a, (src, dst) in enumerate(((corr_in, corr_out), (res_in, res_out))):
        for i in range(parts):
            here = pl.ds(i * size, size)
            copies.append(
                pltpu.make_async_copy(src.at[0, here], dst.at[0, here], sems.at[a, i])
            )
    for copy in copies:
        copy.start()
    for copy in copies:
        copy.wait()


def body(residual_in, self_block, hop_blocks):
    out = jax.ShapeDtypeStruct(residual_in.shape, jnp.float32)
    hbm = pl.BlockSpec(memory_space=pltpu.HBM)
    vmem = pl.BlockSpec(memory_space=pltpu.VMEM)
    tile = (128, 128)
    results = pl.pallas_call(
        kernel,
        out_shape=(out, out),
        in_specs=[hbm] * 3,
        out_specs=(vmem, vmem),
        scratch_shapes=[
            pltpu.VMEM((SITES, 64, 128), jnp.bfloat16),
            pltpu.VMEM((SITES, 8, 64, 128), jnp.bfloat16),
            pltpu.VMEM((SITES, BLOCKS * 128, 128), jnp.bfloat16),
            pltpu.VMEM((STEPS, SITES) + tile, jnp.bfloat16),
            pltpu.VMEM((STEPS, 2, SITES) + tile, jnp.bfloat16),
            pltpu.VMEM((STEPS, 2, PLANE) + tile, jnp.bfloat16),
            pltpu.VMEM((STEPS, GROUPS // 2, SIZE) + tile, jnp.bfloat16),
            pltpu.VMEM((SITES,) + tile, jnp.float32),
            pltpu.SemaphoreType.DMA((3,)),
            pltpu.SemaphoreType.DMA((STEPS, 2)),
            pltpu.SemaphoreType.DMA((STEPS, GROUPS)),
            pltpu.SemaphoreType.DMA((STEPS, GROUPS // 2)),
            pltpu.SemaphoreType.DMA((STEPS,)),
        ],
        compiler_params=pltpu.CompilerParams(
            collective_id=0,
            has_side_effects=True,
            vmem_limit_bytes=48 * 1024 * 1024,
        ),
        name="smoother",
    )(*(pltpu.with_memory_space_constraint(x, pltpu.HBM) for x in (residual_in, self_block, hop_blocks)))
    return pl.pallas_call(
        store,
        out_shape=(out, out),
        in_specs=[pl.BlockSpec(memory_space=pl.ANY)] * 2,
        out_specs=(hbm, hbm),
        scratch_shapes=[pltpu.SemaphoreType.DMA((2, 4))],
        name="store",
    )(*(pltpu.with_memory_space_constraint(x, pltpu.VMEM) for x in results))


def solution(mesh):
    return jax.shard_map(
        body,
        mesh=mesh,
        in_specs=(
            P("site", "group", None, None),
            P("site", None, None, None),
            P("site", None, None, None, None),
        ),
        out_specs=(P("site", "group", None, None), P("site", "group", None, None)),
        check_vma=False,
    )
```
